128 devices in a mesh: ctx: 16 (over y, x_lo, core), head: 8 (over z, x_hi).
Axes of the slice: x: 4 (x_hi: 2, x_lo: 2; x = x_hi * 2 + x_lo), y: 4, z: 4, core: 2. Of those that a mesh axis runs over, the one named last changes fastest.
Arguments:
- activations: bfloat16 [32768, 4096], P('ctx', 'head'), may hold values from -80 to 80
- query_grad: bfloat16 [32768, 4096], P('ctx', 'head'), may hold values from -80 to 80
- example_ids: int32 [32768], P('ctx'), may hold values from 0 to 1, as said below
- band_coefs: bfloat16 [64], replicated, may hold values from 0.049804688 to 1
- noise_history: bfloat16 [64, 4096, 4096], P(None, ('ctx', 'head')), may hold values from -4 to 4
- momentum: float32 [4096, 4096], P(('ctx', 'head')), may hold values from -6 to 6
Outputs:
- momentum_new: float32 [4096, 4096], P(('ctx', 'head'))
- update: bfloat16 [4096, 4096], P('ctx', 'head')
The draws below stay inside these ranges and needn't reach their ends.
Inputs may be any that keep to these rules, and one draw needn't show every extreme that they name: `example_ids`: example 0's tokens come first, then example 1's; each example holds a quarter or more of the 32768 tokens.
All inputs are finite; a program needn't handle non-finite values.
Results may differ from the reference program's by a relative error of at most 0.0085.
Values may be sent and summed in bfloat16 or wider, within the bound.
No kernel may reach another device: no remote copies, remote signals or barrier semaphores. Data moves between devices by JAX's collectives and lax.ppermute only.
A program may use at most 128 MiB of HBM per device.

```python
import math
import jax
import jax.numpy as jnp
from jax import lax

D = 4096
BAND = 64
TOK_DEV = 2048
QW = 4096
TOKENS = 32768
N_CTX = 16


def scaled_matrix(key, row_count, col_count):
    key_list = jax.random.split(key, 3)
    position = jnp.arange(col_count).astype(jnp.float32) / col_count
    col_scale = jnp.exp(math.log(3.0) * position + jax.random.uniform(key_list[1], (col_count,), jnp.float32, 0.0, math.log(10.0)))
    base = jnp.clip(jax.random.normal(key_list[0], (row_count, col_count), jnp.float32), -4.0, 4.0)
    row_scale = jnp.exp(jax.random.uniform(key_list[2], (row_count,), jnp.float32, 0.0, math.log(10.0)))
    return base * row_scale[:, None] * col_scale[None, :] * 0.04


def example_boundary(key):
    return jax.random.randint(jax.random.fold_in(key, 37), (), TOKENS // 4, 3 * TOKENS // 4 + 1)


def draw_activations(key, part):
    return jnp.clip(scaled_matrix(jax.random.fold_in(key, 11), TOKENS, D), -80.0, 80.0).astype(jnp.bfloat16)


def draw_query_grad(key, part):
    raw_grad = scaled_matrix(jax.random.fold_in(key, 23), TOKENS, QW)
    inputs = jnp.clip(scaled_matrix(jax.random.fold_in(key, 11), TOKENS, D), -80.0, 80.0).astype(jnp.bfloat16)
    stride = max(QW // 256, 1)
    sample = raw_grad[:, ::stride]
    sample_cols = sample.shape[1]
    first_rows = (jnp.arange(TOKENS) < example_boundary(key))[:, None]
    split_sample = jnp.concatenate([jnp.where(first_rows, sample, 0.0), jnp.where(first_rows, 0.0, sample)], axis=1).astype(jnp.bfloat16)
    sketch = lax.dot_general(inputs, split_sample, (((0,), (0,)), ((), ())), preferred_element_type=jnp.float32)
    square_first = jnp.sum(sketch[:, :sample_cols] ** 2) * stride
    square_second = jnp.sum(sketch[:, sample_cols:] ** 2) * stride
    rms_first = jnp.sqrt(square_first / (D * QW)) + 1e-30
    rms_second = jnp.sqrt(square_second / (D * QW)) + 1e-30
    small_pick = jax.random.randint(jax.random.fold_in(key, 41), (), 0, 2)
    big_target = jnp.exp(jax.random.uniform(jax.random.fold_in(key, 43), (), jnp.float32, math.log(2.5), math.log(12.0)))
    small_target = jnp.exp(jax.random.uniform(jax.random.fold_in(key, 47), (), jnp.float32, math.log(0.2), math.log(0.45)))
    target_first = jnp.where(small_pick == 0, small_target, big_target)
    target_second = jnp.where(small_pick == 0, big_target, small_target)
    row_factor = jnp.where(first_rows, target_first / rms_first, target_second / rms_second)
    return jnp.clip(raw_grad * row_factor, -80.0, 80.0).astype(jnp.bfloat16)


def draw_example_ids(key, part):
    return (jnp.arange(TOKENS) >= example_boundary(key)).astype(jnp.int32)


def steps_of(key, extent, pieces, low, top_value):
    def one(axis_at, shards_of):
        heights = jax.random.uniform(jax.random.fold_in(jax.random.fold_in(key, 6), axis_at), (shards_of,), jnp.float32, low / len(pieces), top_value / len(pieces))
        return jnp.repeat(jnp.exp(heights), extent[axis_at] // shards_of).reshape((-1,) + (1,) * (len(extent) - axis_at - 1))

    level = one(*pieces[0])
    for cut in pieces[1:]:
        level = level * one(*cut)
    return level


def gaussian(key, dims, width, limit, cuts=(), kind=jnp.bfloat16):
    array = width * jax.random.normal(key, dims, jnp.float32)
    if cuts:
        array = array * steps_of(key, dims, cuts, -0.22, 0.18)
    return jnp.clip(array, -limit, limit).astype(kind)


def setup_inputs(seed: int = 0) -> dict:
    arg_keys = jax.random.split(jax.random.key(seed), 7)
    activations = draw_activations(jax.random.fold_in(arg_keys[6], 71), 0)
    query_grad = draw_query_grad(jax.random.fold_in(arg_keys[6], 71), 0)
    example_ids = draw_example_ids(jax.random.fold_in(arg_keys[6], 71), 0)
    band_coefs = jnp.clip(jnp.exp(jax.random.uniform(arg_keys[3], (BAND,), jnp.float32, math.log(0.049804688), math.log(1.0))), 0.049804688, 1.0).astype(jnp.bfloat16)
    noise_history = gaussian(arg_keys[4], (BAND, D, QW), 1.0, 4.0, ((1, 128),))
    momentum = gaussian(arg_keys[5], (D, QW), 1.0, 6.0, ((0, 128),), jnp.float32)
    return {"activations": activations, "query_grad": query_grad, "example_ids": example_ids, "band_coefs": band_coefs, "noise_history": noise_history, "momentum": momentum}


clip_scale = 1.0
momentum_decay = 0.9
noise_weight = 0.8

def reference(activations, query_grad, example_ids, band_coefs, noise_history, momentum):
    nothing = jnp.zeros((), jnp.bfloat16)
    first_mask = (example_ids == 0)[:, None]
    stacked = jnp.concatenate([jnp.where(first_mask, query_grad, nothing), jnp.where(first_mask, nothing, query_grad)], axis=1)

    def add_block(block_index, running):
        start = (block_index * TOK_DEV).astype(jnp.int32)
        block_rows = lax.dynamic_slice_in_dim(activations, start, TOK_DEV, 0)
        block_grad = lax.dynamic_slice_in_dim(stacked, start, TOK_DEV, 0)
        partial_value = lax.dot_general(block_rows, block_grad, (((0,), (0,)), ((), ())), preferred_element_type=jnp.float32)
        rounded = lax.optimization_barrier(partial_value.astype(jnp.bfloat16))
        return running + rounded.astype(jnp.float32)
    summed = lax.fori_loop(0, N_CTX, add_block, jnp.zeros((D, 2 * QW), jnp.float32))
    grad_first = summed[:, :QW]
    grad_second = summed[:, QW:]
    clip_limit = clip_scale * math.sqrt(D * QW)
    factor_first = clip_limit / jnp.maximum(jnp.sqrt(jnp.sum(grad_first * grad_first)), clip_limit)
    factor_second = clip_limit / jnp.maximum(jnp.sqrt(jnp.sum(grad_second * grad_second)), clip_limit)
    clipped = factor_first * grad_first + factor_second * grad_second
    band_noise = jnp.dot(band_coefs[None, :], noise_history.reshape(BAND, D * QW), preferred_element_type=jnp.float32).reshape(D, QW)
    momentum_new = momentum_decay * momentum + clipped + noise_weight * band_noise
    update = (-(clipped + noise_weight * band_noise + momentum_decay * momentum_new)).astype(jnp.bfloat16)
    return (momentum_new, update)
```

```python
import functools
import math

import jax
import jax.numpy as jnp
from jax import lax
from jax.experimental import pallas as pl
from jax.experimental.pallas import tpu as pltpu
from jax.sharding import PartitionSpec as P

clip_scale = 1.0
momentum_decay = 0.9
noise_weight = 0.8

BOTH = ("ctx", "head")
NY, NXL, NCORE, NZ, NXH = 4, 2, 2, 4, 2
CHUNKS = (128, 128)
TOKEN_BLOCK = 512


def lin(y, xl, core, z, xh):
    return ((y * NXL + xl) * NCORE + core) * (NZ * NXH) + z * NXH + xh


def permute(value, move):
    pairs = []
    for y in range(NY):
        for xl in range(NXL):
            for core in range(NCORE):
                for z in range(NZ):
                    for xh in range(NXH):
                        pairs.append((lin(y, xl, core, z, xh), lin(*move(y, xl, core, z, xh))))
    return lax.ppermute(value, BOTH, pairs)


def swap_core(value):
    return permute(value, lambda y, xl, core, z, xh: (y, xl, 1 - core, z, xh))


def swap_xh(value):
    return permute(value, lambda y, xl, core, z, xh: (y, xl, core, z, 1 - xh))


def swap_xl(value):
    return permute(value, lambda y, xl, core, z, xh: (y, 1 - xl, core, z, xh))


def flip_x(value):
    return permute(value, lambda y, xl, core, z, xh: (y, xh, core, z, xl))


def shift_z(value, step):
    return permute(value, lambda y, xl, core, z, xh: (y, xl, core, (z + step) % NZ, xh))


def shift_y(value, step):
    return permute(value, lambda y, xl, core, z, xh: ((y + step) % NY, xl, core, z, xh))


def product_kernel(
    info, own, up, down, far_a, far_b, q_a, qx_a, q_b, qx_b, plus, minus, late_p, late_m, mine, total
):
    step = pl.program_id(0)
    steps = pl.num_programs(0)
    half = steps // 2
    rows = own.shape[1]
    cols = q_a.shape[1]

    @pl.when(step == 0)
    def _():
        total[...] = jnp.zeros_like(total)

    def add(e, left, qs):
        for i, q in enumerate(qs):
            total[e, :, i * cols : (i + 1) * cols] += jnp.dot(left, q, preferred_element_type=jnp.float32)

    def tokens(base, first_count, far, q, qx):
        left = jnp.concatenate([own[0], up[0], far[...], down[0]], axis=0)
        lo = base * TOKEN_BLOCK

        @pl.when(first_count >= lo + TOKEN_BLOCK)
        def _():
            add(0, left, (q[...], qx[...]))

        @pl.when(first_count <= lo)
        def _():
            add(1, left, (q[...], qx[...]))

        @pl.when(jnp.logical_and(first_count > lo, first_count < lo + TOKEN_BLOCK))
        def _():
            is_first = lax.broadcasted_iota(jnp.int32, q.shape, 0) < first_count - lo
            nothing = jnp.zeros(q.shape, q.dtype)
            add(0, left, [jnp.where(is_first, r[...], nothing) for r in (q, qx)])
            add(1, left, [jnp.where(is_first, nothing, r[...]) for r in (q, qx)])

    @pl.when(step < half)
    def _():
        tokens(step, info[0], far_a, q_a, qx_a)

    @pl.when(step >= half)
    def _():
        tokens(step - half, info[1], far_b, q_b, qx_b)

    @pl.when(step == steps - 1)
    def _():
        def block(r, e):
            k = jnp.bitwise_and(info[2] - r, NZ - 1)
            return total[e, pl.ds(pl.multiple_of(k * rows, rows), rows), :].astype(jnp.bfloat16)

        plus[0] = block(2, 0)
        plus[1] = block(1, 1)
        minus[0] = block(3, 0)
        minus[1] = block(2, 1)
        late_p[...] = block(1, 0)
        late_m[...] = block(3, 1)
        mine[0] = block(0, 0)
        mine[1] = block(0, 1)


def product(info, own, up, down, far_a, far_b, q_a, qx_a, q_b, qx_b):
    rows, tokens = own.shape[1], own.shape[2]
    cols = q_a.shape[1]
    half = tokens // TOKEN_BLOCK
    left3 = pl.BlockSpec((1, rows, TOKEN_BLOCK), lambda s, info: (s // half, 0, s % half))
    first = lambda s: jnp.minimum(s, half - 1)
    second = lambda s: jnp.maximum(s - half, 0)
    in_specs = [
        left3,
        left3,
        left3,
        pl.BlockSpec((rows, TOKEN_BLOCK), lambda s, info: (0, first(s))),
        pl.BlockSpec((rows, TOKEN_BLOCK), lambda s, info: (0, second(s))),
        pl.BlockSpec((TOKEN_BLOCK, cols), lambda s, info: (first(s), 0)),
        pl.BlockSpec((TOKEN_BLOCK, cols), lambda s, info: (first(s), 0)),
        pl.BlockSpec((TOKEN_BLOCK, cols), lambda s, info: (second(s), 0)),
        pl.BlockSpec((TOKEN_BLOCK, cols), lambda s, info: (second(s), 0)),
    ]
    pair = jax.ShapeDtypeStruct((2, rows, 2 * cols), jnp.bfloat16)
    single = jax.ShapeDtypeStruct((rows, 2 * cols), jnp.bfloat16)
    pair_spec = pl.BlockSpec((2, rows, 2 * cols), lambda s, info: (0, 0, 0))
    single_spec = pl.BlockSpec((rows, 2 * cols), lambda s, info: (0, 0))
    return pl.pallas_call(
        product_kernel,
        grid_spec=pltpu.PrefetchScalarGridSpec(
            num_scalar_prefetch=1,
            grid=(2 * half,),
            in_specs=in_specs,
            out_specs=[pair_spec, pair_spec, single_spec, single_spec, pair_spec],
            scratch_shapes=[pltpu.VMEM((2, NZ * rows, 2 * cols), jnp.float32)],
        ),
        out_shape=[pair, pair, single, single, pair],
        cost_estimate=pl.CostEstimate(
            flops=2 * 2 * tokens * NZ * rows * 2 * cols,
            bytes_accessed=2 * (2 * tokens * (NZ * rows + 2 * cols) + 8 * rows * 2 * cols),
            transcendentals=0,
        ),
        compiler_params=pltpu.CompilerParams(vmem_limit_bytes=48 * 1024 * 1024),
        name="product",
    )(info, own, up, down, far_a, far_b, q_a, qx_a, q_b, qx_b)


def local(activations, query_grad, example_ids, band_coefs, noise_history, momentum):
    f32, bf16 = jnp.float32, jnp.bfloat16
    ctx, head = lax.axis_index("ctx"), lax.axis_index("head")
    y, xl, core = ctx // (NXL * NCORE), (ctx // NCORE) % NXL, ctx % NCORE
    z, xh = head // NXH, head % NXH
    head_cols = query_grad.shape[1]
    half_cols = activations.shape[1] // NCORE

    first_count = jnp.sum((example_ids == 0).astype(jnp.int32)).reshape(1)
    other_count = swap_core(first_count)
    info = jnp.concatenate([first_count, other_count, ((z - y) % NZ).reshape(1).astype(jnp.int32)])

    turned = activations.T
    keep = lax.dynamic_slice_in_dim(turned, core * half_cols, half_cols, 0)
    give = lax.dynamic_slice_in_dim(turned, (1 - core) * half_cols, half_cols, 0)
    left = jnp.stack([keep, swap_core(give)])

    qx = swap_xh(query_grad)
    q_other = swap_core(query_grad)
    qx_other = swap_core(qx)

    noise = jnp.sum(band_coefs.astype(f32)[:, None, None] * noise_history.astype(f32), axis=0)
    base = momentum_decay * momentum + noise_weight * noise
    ahead = ((1.0 + momentum_decay) * noise_weight * noise + momentum_decay**2 * momentum).astype(bf16)
    owner_rows = ahead.shape[0]
    ahead = lax.all_to_all(
        ahead.reshape(owner_rows, NZ * NXH, head_cols), "head", split_axis=1, concat_axis=0, tiled=True
    ).reshape(-1, head_cols)

    done = []
    start = 0
    for rows in CHUNKS:
        piece = left[:, start : start + rows]
        start += rows
        up = shift_z(piece, 1)
        down = shift_z(piece, -1)
        far_a = shift_z(up[0], 1)
        far_b = shift_z(down[1], -1)
        plus, minus, late_p, late_m, mine = product(
            info, piece, up, down, far_a, far_b, query_grad, qx, q_other, qx_other
        )
        from_below = shift_y(plus, 1)
        from_above = shift_y(minus, -1)
        late_p = (late_p.astype(f32) + from_below[0].astype(f32)).astype(bf16)
        late_m = (late_m.astype(f32) + from_above[1].astype(f32)).astype(bf16)
        got_p = shift_y(late_p, 1)
        got_m = shift_y(late_m, -1)
        sum_first = mine[0].astype(f32) + got_p.astype(f32) + from_above[0].astype(f32)
        sum_second = mine[1].astype(f32) + from_below[1].astype(f32) + got_m.astype(f32)
        sums = jnp.stack([sum_first, sum_second])
        side = jnp.bitwise_xor(xl, xh)
        kept = lax.dynamic_slice_in_dim(sums, side * head_cols, head_cols, 2)
        sent = lax.dynamic_slice_in_dim(sums, (1 - side) * head_cols, head_cols, 2).astype(bf16)
        done.append(kept + swap_xl(sent).astype(f32))

    grads = jnp.concatenate(done, axis=1)
    squares = jnp.sum(grads * grads, axis=(1, 2))
    count = lax.axis_size("ctx") * lax.axis_size("head")
    lanes = jnp.zeros((128,), f32).at[:2].set(squares)
    all_squares = lax.all_to_all(jnp.broadcast_to(lanes, (count, 128)), BOTH, 0, 0, tiled=True)
    norm_sums = jnp.sum(all_squares[:, :2], axis=0)

    cols_own = flip_x(grads.astype(bf16))
    rows_own = lax.all_to_all(
        cols_own.reshape(2, NZ * NXH, owner_rows, head_cols), "head", split_axis=1, concat_axis=3, tiled=True
    ).reshape(2, owner_rows, -1)

    clip_limit = clip_scale * math.sqrt(momentum.shape[1] * NZ * NXH * head_cols)
    factors = clip_limit / jnp.maximum(jnp.sqrt(norm_sums), clip_limit)
    momentum_new = base + factors[0] * rows_own[0].astype(f32) + factors[1] * rows_own[1].astype(f32)
    clipped = factors[0] * cols_own[0].astype(f32) + factors[1] * cols_own[1].astype(f32)
    update = (-((1.0 + momentum_decay) * clipped + ahead.astype(f32))).astype(bf16)
    return (momentum_new, update)


def solution(mesh):
    in_specs = (
        P("ctx", "head"),
        P("ctx", "head"),
        P("ctx"),
        P(),
        P(None, ("ctx", "head"), None),
        P(("ctx", "head"), None),
    )
    out_specs = (P(("ctx", "head"), None), P("ctx", "head"))
    return jax.shard_map(local, mesh=mesh, in_specs=in_specs, out_specs=out_specs, check_vma=False)
```

```python
import math

import jax
import jax.numpy as jnp
from jax import lax
from jax.experimental import pallas as pl
from jax.experimental.pallas import tpu as pltpu
from jax.sharding import PartitionSpec as P


clip_scale = 1.0
momentum_decay = 0.9
noise_weight = 0.8

BOTH = ("ctx", "head")
NY, NXL, NCORE, NZ, NXH = 4, 2, 2, 4, 2
CHUNKS = (160, 96)
TOKEN_BLOCK = 1024
SPLIT = 2


def lin(y, xl, core, z, xh):
    return ((y * NXL + xl) * NCORE + core) * (NZ * NXH) + z * NXH + xh


def permute(value, move):
    pairs = []
    for y in range(NY):
        for xl in range(NXL):
            for core in range(NCORE):
                for z in range(NZ):
                    for xh in range(NXH):
                        pairs.append((lin(y, xl, core, z, xh), lin(*move(y, xl, core, z, xh))))
    return lax.ppermute(value, BOTH, pairs)


def swap_core(value):
    return permute(value, lambda y, xl, core, z, xh: (y, xl, 1 - core, z, xh))


def swap_xh(value):
    return permute(value, lambda y, xl, core, z, xh: (y, xl, core, z, 1 - xh))


def swap_xl(value):
    return permute(value, lambda y, xl, core, z, xh: (y, 1 - xl, core, z, xh))


def gather_x(value):
    def move(y, xl, core, z, xh):
        to = {0: 2, 1: 0, 2: 3, 3: 1}[NXL * xh + xl]
        return y, to % NXL, core, z, to // NXL

    return permute(value, move)


def cross_x(value):
    def move(y, xl, core, z, xh):
        to = {0: 3, 1: 2, 2: 1, 3: 0}[NXL * xh + xl]
        return y, to % NXL, core, z, to // NXL

    return permute(value, move)


def shift_z(value, step):
    return permute(value, lambda y, xl, core, z, xh: (y, xl, core, (z + step) % NZ, xh))


def shift_y(value, step):
    return permute(value, lambda y, xl, core, z, xh: ((y + step) % NY, xl, core, z, xh))


def turn_kernel(core, keep, give, *outs):
    kept, given = keep[...].T, give[...].T
    start = 0
    for i, rows in enumerate(CHUNKS):
        outs[2 * i][...] = kept[start : start + rows]
        outs[2 * i + 1][...] = given[start : start + rows]
        start += rows


def turn(core, activations):
    tokens, width = activations.shape
    half = width // NCORE
    block = 1024
    shapes, specs = [], []
    for rows in CHUNKS:
        for _ in range(2):
            shapes.append(jax.ShapeDtypeStruct((rows, tokens), activations.dtype))
            specs.append(pl.BlockSpec((rows, block), lambda i, core: (0, i)))
    return pl.pallas_call(
        turn_kernel,
        grid_spec=pltpu.PrefetchScalarGridSpec(
            num_scalar_prefetch=1,
            grid=(tokens // block,),
            in_specs=[
                pl.BlockSpec((block, half), lambda i, core: (i, core[0])),
                pl.BlockSpec((block, half), lambda i, core: (i, 1 - core[0])),
            ],
            out_specs=specs,
        ),
        out_shape=shapes,
        cost_estimate=pl.CostEstimate(flops=0, bytes_accessed=4 * tokens * width, transcendentals=0),
        compiler_params=pltpu.CompilerParams(vmem_limit_bytes=60 * 1024 * 1024),
        name="turn",
    )(core, activations, activations)


def product_kernel(count_a, count_b, origin, *refs):
    sources, queries, outs = refs[0:8], refs[8:12], refs[13:18]
    left, right, total, plus, minus, late_p, late_m, mine, left_sem, right_sem, out_sem = refs[18:]
    rows = sources[0].shape[0]
    tokens, cols = queries[0].shape
    blocks = tokens // TOKEN_BLOCK

    def left_copy(half, k):
        target = left.at[half, pl.ds(k * rows, rows)]
        return pltpu.make_async_copy(sources[half * NZ + k], target, left_sem.at[half, k])

    def right_copy(half, side, j):
        at = pl.ds(j * TOKEN_BLOCK, TOKEN_BLOCK)
        source = queries[half * 2 + side].at[at]
        target = right.at[half, at, pl.ds(side * cols, cols)]
        return pltpu.make_async_copy(source, target, right_sem.at[half, side, j])

    for half in range(2):
        for k in range(NZ):
            left_copy(half, k).start()
        for j in range(blocks):
            for side in range(2):
                right_copy(half, side, j).start()

    total[...] = jnp.zeros_like(total)

    def add(half, first_count, lo, size):
        at = pl.ds(pl.multiple_of(lo, size), size)
        e = jnp.where(first_count <= lo, 1, 0)
        total[e] += jnp.dot(left[half, :, at], right[half, at, :], preferred_element_type=jnp.float32)

    def is_mixed(first_count, lo, size):
        return jnp.logical_and(first_count > lo, first_count < lo + size)

    for half in range(2):
        first_count = (count_a, count_b)[half][0]
        for k in range(NZ):
            left_copy(half, k).wait()
        for j in range(blocks):
            for side in range(2):
                right_copy(half, side, j).wait()
            lo = j * TOKEN_BLOCK
            mixed = is_mixed(first_count, lo, TOKEN_BLOCK)

            @pl.when(jnp.logical_not(mixed))
            def _(half=half, lo=lo, first_count=first_count):
                add(half, first_count, lo, TOKEN_BLOCK)

            @pl.when(mixed)
            def _(half=half, lo=lo, first_count=first_count):
                size = TOKEN_BLOCK // SPLIT

                def one(i, carry):
                    low = lo + i * size
                    inner = is_mixed(first_count, low, size)

                    @pl.when(jnp.logical_not(inner))
                    def _():
                        add(half, first_count, low, size)

                    @pl.when(inner)
                    def _():
                        at = pl.ds(pl.multiple_of(low, size), size)
                        query = right[half, at, :]
                        is_first = lax.broadcasted_iota(jnp.int32, query.shape, 0) < first_count - low
                        nothing = jnp.zeros_like(query)
                        value = left[half, :, at]
                        for e, pick in enumerate((jnp.where(is_first, query, nothing), jnp.where(is_first, nothing, query))):
                            total[e] += jnp.dot(value, pick, preferred_element_type=jnp.float32)

                    return carry

                lax.fori_loop(0, SPLIT, one, 0)

    def block(r, e):
        k = jnp.bitwise_and(origin[0] - r, NZ - 1)
        return total[e, pl.ds(pl.multiple_of(k * rows, rows), rows), :].astype(jnp.bfloat16)

    def out_copy(i):
        return pltpu.make_async_copy((plus, minus, late_p, late_m, mine)[i], outs[i], out_sem.at[i])

    plus[0] = block(2, 0)
    plus[1] = block(1, 1)
    out_copy(0).start()
    minus[0] = block(3, 0)
    minus[1] = block(2, 1)
    out_copy(1).start()
    late_p[...] = block(1, 0)
    out_copy(2).start()
    late_m[...] = block(3, 1)
    out_copy(3).start()
    mine[0] = block(0, 0)
    mine[1] = block(0, 1)
    out_copy(4).start()
    for i in range(5):
        out_copy(i).wait()


def product(info, left_a, left_b, q_a, qx_a, q_b, qx_b, after):
    rows, tokens = left_a[0].shape
    cols = q_a.shape[1]
    pair, single = (2, rows, 2 * cols), (rows, 2 * cols)
    shapes = [pair, pair, single, single, pair]
    smem = pl.BlockSpec(memory_space=pltpu.SMEM)
    anywhere = pl.BlockSpec(memory_space=pl.ANY)
    return pl.pallas_call(
        product_kernel,
        in_specs=[smem] * 3 + [anywhere] * 13,
        out_specs=[anywhere] * 5,
        out_shape=[jax.ShapeDtypeStruct(shape, jnp.bfloat16) for shape in shapes],
        scratch_shapes=[
            pltpu.VMEM((2, NZ * rows, tokens), jnp.bfloat16),
            pltpu.VMEM((2, tokens, 2 * cols), jnp.bfloat16),
            pltpu.VMEM((2, NZ * rows, 2 * cols), jnp.float32),
        ]
        + [pltpu.VMEM(shape, jnp.bfloat16) for shape in shapes]
        + [
            pltpu.SemaphoreType.DMA((2, NZ)),
            pltpu.SemaphoreType.DMA((2, 2, tokens // TOKEN_BLOCK)),
            pltpu.SemaphoreType.DMA((5,)),
        ],
        cost_estimate=pl.CostEstimate(
            flops=2 * 2 * tokens * NZ * rows * 2 * cols,
            bytes_accessed=2 * (2 * tokens * (NZ * rows + 2 * cols) + 8 * rows * 2 * cols),
            transcendentals=0,
        ),
        compiler_params=pltpu.CompilerParams(vmem_limit_bytes=60 * 1024 * 1024),
        name="product",
    )(*info, *left_a, *left_b, q_a, qx_a, q_b, qx_b, after)


def finish_kernel(
    info, squares, part_0, part_1, part_2, part_3, base, grads, flipped, ahead, momentum_new, update
):
    limit = clip_scale * math.sqrt(base.shape[1] * base.shape[1])
    sums = jnp.sum(squares[...], axis=0, keepdims=True)
    factors = limit / jnp.maximum(jnp.sqrt(sums), limit)
    cols = grads.shape[2]
    wide = [jnp.concatenate([factors[:, e * 128 : (e + 1) * 128]] * (cols // 128), axis=1) for e in range(2)]
    for k, part in enumerate((part_0, part_1, part_2, part_3)):
        origin = jnp.bitwise_and(info[0] - k, NZ - 1)
        for i, half in enumerate((info[1], 1 - info[1])):
            at = pl.ds(pl.multiple_of((origin * NXH + half) * cols, cols), cols)
            first = wide[0] * part[i, 0].astype(jnp.float32)
            second = wide[1] * part[i, 1].astype(jnp.float32)
            momentum_new[:, at] = base[:, at] + first + second

    def write(first, second):
        clipped = wide[0] * first + wide[1] * second
        total = (1.0 + momentum_decay) * clipped + ahead[...].astype(jnp.float32)
        update[...] = (-total).astype(jnp.bfloat16)

    @pl.when(info[2] == 1)
    def _():
        write(grads[0], grads[1])

    @pl.when(info[2] == 0)
    def _():
        write(flipped[0].astype(jnp.float32), flipped[1].astype(jnp.float32))


def finish(info, squares, parts, base, grads, flipped, ahead):
    return pl.pallas_call(
        finish_kernel,
        in_specs=[pl.BlockSpec(memory_space=pltpu.SMEM)] + [pl.BlockSpec(memory_space=pltpu.VMEM)] * 9,
        out_specs=[pl.BlockSpec(memory_space=pltpu.VMEM)] * 2,
        out_shape=[
            jax.ShapeDtypeStruct(base.shape, jnp.float32),
            jax.ShapeDtypeStruct(ahead.shape, jnp.bfloat16),
        ],
        compiler_params=pltpu.CompilerParams(vmem_limit_bytes=16 * 1024 * 1024),
        name="finish",
    )(info, squares, *parts, base, grads, flipped, ahead)


def step(activations, query_grad, example_ids, band_coefs, noise_history, momentum):
    f32, bf16 = jnp.float32, jnp.bfloat16
    ctx, head = lax.axis_index("ctx"), lax.axis_index("head")
    y, xl, core = ctx >> 2, (ctx >> 1) & 1, ctx & 1
    z, xh = head >> 1, head & 1
    head_cols = query_grad.shape[1]

    first_count = jnp.sum((example_ids == 0).astype(jnp.int32)).reshape(1)
    other_count = swap_core(first_count)
    info = (first_count, other_count, (z - y + NZ).reshape(1).astype(jnp.int32))

    pieces = turn(core.reshape(1).astype(jnp.int32), activations)

    qx = swap_xh(query_grad)
    q_other = swap_core(query_grad)
    qx_other = swap_core(qx)

    noise = jnp.sum(band_coefs.astype(f32)[:, None, None] * noise_history.astype(f32), axis=0)
    base = momentum_decay * momentum + noise_weight * noise
    ahead = ((1.0 + momentum_decay) * noise_weight * noise + momentum_decay**2 * momentum).astype(bf16)
    owner_rows = ahead.shape[0]
    ahead = ahead.reshape(owner_rows, NZ * NXH, head_cols).transpose(1, 0, 2)
    ahead = lax.all_to_all(ahead, "head", split_axis=0, concat_axis=0, tiled=True)
    ahead = ahead.reshape(-1, head_cols)

    same = xl == xh
    done = []
    for i in range(len(CHUNKS)):
        own = pieces[2 * i]
        taken = swap_core(pieces[2 * i + 1])
        up_own = shift_z(own, 1)
        up_taken = shift_z(taken, 1)
        down_taken = shift_z(taken, -1)
        down_own = shift_z(own, -1)
        far_own = shift_z(up_own, 1)
        far_taken = shift_z(down_taken, -1)
        plus, minus, late_p, late_m, mine = product(
            info,
            (own, up_own, far_own, down_own),
            (taken, up_taken, far_taken, down_taken),
            query_grad,
            qx,
            q_other,
            qx_other,
            ahead,
        )
        from_below = shift_y(plus, 1)
        from_above = shift_y(minus, -1)
        late_p = (late_p.astype(f32) + from_below[0].astype(f32)).astype(bf16)
        late_m = (late_m.astype(f32) + from_above[1].astype(f32)).astype(bf16)
        got_p = shift_y(late_p, 1)
        got_m = shift_y(late_m, -1)
        sum_first = mine[0].astype(f32) + got_p.astype(f32) + from_above[0].astype(f32)
        sum_second = mine[1].astype(f32) + from_below[1].astype(f32) + got_m.astype(f32)
        near = jnp.stack([sum_first[:, :head_cols], sum_second[:, :head_cols]])
        other = jnp.stack([sum_first[:, head_cols:], sum_second[:, head_cols:]])
        got = swap_xl(jnp.where(same, other, near).astype(bf16))
        total = got.astype(f32) + jnp.where(same, near, other)
        done.append(total)

    grads = jnp.concatenate(done, axis=1)
    squares = sum(jnp.sum(d * d, axis=(1, 2)) for d in done)
    count = lax.axis_size("ctx") * lax.axis_size("head")
    lanes = jnp.repeat(squares, 128)[None, :]
    all_squares = lax.all_to_all(jnp.broadcast_to(lanes, (count, 256)), BOTH, 0, 0, tiled=True)

    narrow = grads.astype(bf16)
    blocks = narrow.reshape(2, NZ, NXH, owner_rows, head_cols)
    far = gather_x(jnp.where(xl == 0, blocks[:, :, 1], blocks[:, :, 0]))
    near = jnp.where(xl == 0, blocks[:, :, 0], blocks[:, :, 1])
    near = jnp.where(same, near, cross_x(near))
    flipped = cross_x(narrow)
    both = jnp.stack([near, far])
    parts = [lax.dynamic_index_in_dim(both, z, 2, False)]
    for k in range(1, NZ):
        parts.append(shift_z(lax.dynamic_index_in_dim(both, (z + k) & (NZ - 1), 2, False), k))
    facts = jnp.stack([z, xh, same.astype(z.dtype)]).astype(jnp.int32)
    return finish(facts, all_squares, parts, base, grads, flipped, ahead)


def solution(mesh):
    in_specs = (
        P("ctx", "head"),
        P("ctx", "head"),
        P("ctx"),
        P(),
        P(None, ("ctx", "head"), None),
        P(("ctx", "head"), None),
    )
    out_specs = (P(("ctx", "head"), None), P("ctx", "head"))
    return jax.shard_map(step, mesh=mesh, in_specs=in_specs, out_specs=out_specs, check_vma=False)
```

```python
import math

import jax
import jax.numpy as jnp
from jax import lax
from jax.experimental import pallas as pl
from jax.experimental.pallas import tpu as pltpu
from jax.sharding import PartitionSpec as P


clip_scale = 1.0
momentum_decay = 0.9
noise_weight = 0.8

BOTH = ("ctx", "head")
NY, NXL, NCORE, NZ, NXH = 4, 2, 2, 4, 2
CHUNKS = (160, 96)
TOKEN_BLOCK = 1024
SPLIT = 2


def lin(y, xl, core, z, xh):
    return ((y * NXL + xl) * NCORE + core) * (NZ * NXH) + z * NXH + xh


def permute(value, move):
    pairs = []
    for y in range(NY):
        for xl in range(NXL):
            for core in range(NCORE):
                for z in range(NZ):
                    for xh in range(NXH):
                        pairs.append((lin(y, xl, core, z, xh), lin(*move(y, xl, core, z, xh))))
    return lax.ppermute(value, BOTH, pairs)


def swap_core(value):
    return permute(value, lambda y, xl, core, z, xh: (y, xl, 1 - core, z, xh))


def swap_xh(value):
    return permute(value, lambda y, xl, core, z, xh: (y, xl, core, z, 1 - xh))


def swap_xl(value):
    return permute(value, lambda y, xl, core, z, xh: (y, 1 - xl, core, z, xh))


def gather_x(value):
    def move(y, xl, core, z, xh):
        to = {0: 2, 1: 0, 2: 3, 3: 1}[NXL * xh + xl]
        return y, to % NXL, core, z, to // NXL

    return permute(value, move)


def cross_x(value):
    def move(y, xl, core, z, xh):
        to = {0: 3, 1: 2, 2: 1, 3: 0}[NXL * xh + xl]
        return y, to % NXL, core, z, to // NXL

    return permute(value, move)


def shift_z(value, step):
    return permute(value, lambda y, xl, core, z, xh: (y, xl, core, (z + step) % NZ, xh))


def shift_y(value, step):
    return permute(value, lambda y, xl, core, z, xh: ((y + step) % NY, xl, core, z, xh))


def turn_kernel(core, keep, give, *outs):
    kept, given = keep[...].T, give[...].T
    start = 0
    for i, rows in enumerate(CHUNKS):
        outs[2 * i][...] = kept[start : start + rows]
        outs[2 * i + 1][...] = given[start : start + rows]
        start += rows


def turn(core, activations):
    tokens, width = activations.shape
    half = width // NCORE
    block = 1024
    shapes, specs = [], []
    for rows in CHUNKS:
        for _ in range(2):
            shapes.append(jax.ShapeDtypeStruct((rows, tokens), activations.dtype))
            specs.append(pl.BlockSpec((rows, block), lambda i, core: (0, i)))
    return pl.pallas_call(
        turn_kernel,
        grid_spec=pltpu.PrefetchScalarGridSpec(
            num_scalar_prefetch=1,
            grid=(tokens // block,),
            in_specs=[
                pl.BlockSpec((block, half), lambda i, core: (i, core[0])),
                pl.BlockSpec((block, half), lambda i, core: (i, 1 - core[0])),
            ],
            out_specs=specs,
        ),
        out_shape=shapes,
        cost_estimate=pl.CostEstimate(flops=0, bytes_accessed=4 * tokens * width, transcendentals=0),
        compiler_params=pltpu.CompilerParams(vmem_limit_bytes=60 * 1024 * 1024),
        name="turn",
    )(core, activations, activations)


def product_kernel(count_a, count_b, origin, *refs):
    sources, queries, outs = refs[0:8], refs[8:12], refs[13:18]
    left, right, total, plus, minus, late_p, late_m, mine, left_sem, right_sem, out_sem = refs[18:]
    rows = sources[0].shape[0]
    tokens, cols = queries[0].shape
    blocks = tokens // TOKEN_BLOCK

    def left_copy(half, k):
        target = left.at[half, pl.ds(k * rows, rows)]
        return pltpu.make_async_copy(sources[half * NZ + k], target, left_sem.at[half, k])

    def right_copy(half, side, j):
        at = pl.ds(j * TOKEN_BLOCK, TOKEN_BLOCK)
        source = queries[half * 2 + side].at[at]
        target = right.at[half, at, pl.ds(side * cols, cols)]
        return pltpu.make_async_copy(source, target, right_sem.at[half, side, j])

    for half in range(2):
        for k in range(NZ):
            left_copy(half, k).start()
        for j in range(blocks):
            for side in range(2):
                right_copy(half, side, j).start()

    total[...] = jnp.zeros_like(total)

    def add(half, first_count, lo, size):
        at = pl.ds(pl.multiple_of(lo, size), size)
        e = jnp.where(first_count <= lo, 1, 0)
        total[e] += jnp.dot(left[half, :, at], right[half, at, :], preferred_element_type=jnp.float32)

    def is_mixed(first_count, lo, size):
        return jnp.logical_and(first_count > lo, first_count < lo + size)

    def chunk(t, carry):
        half, j = t // blocks, t % blocks
        first_count = jnp.where(half == 0, count_a[0], count_b[0])

        @pl.when(j == 0)
        def _():
            for k in range(NZ):
                target = left.at[half, pl.ds(k * rows, rows)]
                pltpu.make_async_copy(sources[k], target, left_sem.at[half, k]).wait()

        lo = pl.multiple_of(j * TOKEN_BLOCK, TOKEN_BLOCK)
        for side in range(2):
            target = right.at[half, pl.ds(lo, TOKEN_BLOCK), pl.ds(side * cols, cols)]
            source = queries[side].at[pl.ds(lo, TOKEN_BLOCK)]
            pltpu.make_async_copy(source, target, right_sem.at[half, side, j]).wait()
        mixed = is_mixed(first_count, lo, TOKEN_BLOCK)

        @pl.when(jnp.logical_not(mixed))
        def _():
            add(half, first_count, lo, TOKEN_BLOCK)

        @pl.when(mixed)
        def _():
            size = TOKEN_BLOCK // SPLIT

            def one(i, inner_carry):
                low = lo + i * size
                at = pl.ds(pl.multiple_of(low, size), size)
                query = right[half, at, :]
                is_first = lax.broadcasted_iota(jnp.int32, query.shape, 0) < first_count - low
                nothing = jnp.zeros_like(query)
                value = left[half, :, at]

                @pl.when(first_count > low)
                def _():
                    total[0] += jnp.dot(value, jnp.where(is_first, query, nothing), preferred_element_type=jnp.float32)

                @pl.when(first_count < low + size)
                def _():
                    total[1] += jnp.dot(value, jnp.where(is_first, nothing, query), preferred_element_type=jnp.float32)

                return inner_carry

            lax.fori_loop(0, SPLIT, one, 0)

        return carry

    lax.fori_loop(0, 2 * blocks, chunk, 0)

    def block(r, e):
        k = jnp.bitwise_and(origin[0] - r, NZ - 1)
        return total[e, pl.ds(pl.multiple_of(k * rows, rows), rows), :].astype(jnp.bfloat16)

    def out_copy(i):
        return pltpu.make_async_copy((plus, minus, late_p, late_m, mine)[i], outs[i], out_sem.at[i])

    plus[0] = block(2, 0)
    plus[1] = block(1, 1)
    out_copy(0).start()
    minus[0] = block(3, 0)
    minus[1] = block(2, 1)
    out_copy(1).start()
    late_p[...] = block(1, 0)
    out_copy(2).start()
    late_m[...] = block(3, 1)
    out_copy(3).start()
    mine[0] = block(0, 0)
    mine[1] = block(0, 1)
    out_copy(4).start()
    for i in range(5):
        out_copy(i).wait()


def product(info, left_a, left_b, q_a, qx_a, q_b, qx_b, after):
    rows, tokens = left_a[0].shape
    cols = q_a.shape[1]
    pair, single = (2, rows, 2 * cols), (rows, 2 * cols)
    shapes = [pair, pair, single, single, pair]
    smem = pl.BlockSpec(memory_space=pltpu.SMEM)
    anywhere = pl.BlockSpec(memory_space=pl.ANY)
    return pl.pallas_call(
        product_kernel,
        in_specs=[smem] * 3 + [anywhere] * 13,
        out_specs=[anywhere] * 5,
        out_shape=[jax.ShapeDtypeStruct(shape, jnp.bfloat16) for shape in shapes],
        scratch_shapes=[
            pltpu.VMEM((2, NZ * rows, tokens), jnp.bfloat16),
            pltpu.VMEM((2, tokens, 2 * cols), jnp.bfloat16),
            pltpu.VMEM((2, NZ * rows, 2 * cols), jnp.float32),
        ]
        + [pltpu.VMEM(shape, jnp.bfloat16) for shape in shapes]
        + [
            pltpu.SemaphoreType.DMA((2, NZ)),
            pltpu.SemaphoreType.DMA((2, 2, tokens // TOKEN_BLOCK)),
            pltpu.SemaphoreType.DMA((5,)),
        ],
        cost_estimate=pl.CostEstimate(
            flops=2 * 2 * tokens * NZ * rows * 2 * cols,
            bytes_accessed=2 * (2 * tokens * (NZ * rows + 2 * cols) + 8 * rows * 2 * cols),
            transcendentals=0,
        ),
        compiler_params=pltpu.CompilerParams(vmem_limit_bytes=60 * 1024 * 1024),
        name="product",
    )(*info, *left_a, *left_b, q_a, qx_a, q_b, qx_b, after)


def finish_kernel(
    info, squares, part_0, part_1, part_2, part_3, base, grads, flipped, ahead, momentum_new, update
):
    limit = clip_scale * math.sqrt(base.shape[1] * base.shape[1])
    sums = jnp.sum(squares[...], axis=0, keepdims=True)
    factors = limit / jnp.maximum(jnp.sqrt(sums), limit)
    cols = grads.shape[2]
    wide = [jnp.concatenate([factors[:, e * 128 : (e + 1) * 128]] * (cols // 128), axis=1) for e in range(2)]
    for k, part in enumerate((part_0, part_1, part_2, part_3)):
        origin = jnp.bitwise_and(info[0] - k, NZ - 1)
        for i, half in enumerate((info[1], 1 - info[1])):
            at = pl.ds(pl.multiple_of((origin * NXH + half) * cols, cols), cols)
            first = wide[0] * part[i, 0].astype(jnp.float32)
            second = wide[1] * part[i, 1].astype(jnp.float32)
            momentum_new[:, at] = base[:, at] + first + second

    def write(first, second):
        clipped = wide[0] * first + wide[1] * second
        total = (1.0 + momentum_decay) * clipped + ahead[...].astype(jnp.float32)
        update[...] = (-total).astype(jnp.bfloat16)

    @pl.when(info[2] == 1)
    def _():
        write(grads[0], grads[1])

    @pl.when(info[2] == 0)
    def _():
        write(flipped[0].astype(jnp.float32), flipped[1].astype(jnp.float32))


def finish(info, squares, parts, base, grads, flipped, ahead):
    return pl.pallas_call(
        finish_kernel,
        in_specs=[pl.BlockSpec(memory_space=pltpu.SMEM)] + [pl.BlockSpec(memory_space=pltpu.VMEM)] * 9,
        out_specs=[pl.BlockSpec(memory_space=pltpu.VMEM)] * 2,
        out_shape=[
            jax.ShapeDtypeStruct(base.shape, jnp.float32),
            jax.ShapeDtypeStruct(ahead.shape, jnp.bfloat16),
        ],
        compiler_params=pltpu.CompilerParams(vmem_limit_bytes=16 * 1024 * 1024),
        name="finish",
    )(info, squares, *parts, base, grads, flipped, ahead)


def step(activations, query_grad, example_ids, band_coefs, noise_history, momentum):
    f32, bf16 = jnp.float32, jnp.bfloat16
    ctx, head = lax.axis_index("ctx"), lax.axis_index("head")
    y, xl, core = ctx >> 2, (ctx >> 1) & 1, ctx & 1
    z, xh = head >> 1, head & 1
    head_cols = query_grad.shape[1]

    first_count = jnp.sum((example_ids == 0).astype(jnp.int32)).reshape(1)
    other_count = swap_core(first_count)
    info = (first_count, other_count, (z - y + NZ).reshape(1).astype(jnp.int32))

    pieces = turn(core.reshape(1).astype(jnp.int32), activations)

    qx = swap_xh(query_grad)
    q_other = swap_core(query_grad)
    qx_other = swap_core(qx)

    noise = jnp.sum(band_coefs.astype(f32)[:, None, None] * noise_history.astype(f32), axis=0)
    base = momentum_decay * momentum + noise_weight * noise
    ahead = ((1.0 + momentum_decay) * noise_weight * noise + momentum_decay**2 * momentum).astype(bf16)
    owner_rows = ahead.shape[0]
    ahead = ahead.reshape(owner_rows, NZ * NXH, head_cols).transpose(1, 0, 2)
    ahead = lax.all_to_all(ahead, "head", split_axis=0, concat_axis=0, tiled=True)
    ahead = ahead.reshape(-1, head_cols)

    same = xl == xh
    done = []
    for i in range(len(CHUNKS)):
        own = pieces[2 * i]
        taken = swap_core(pieces[2 * i + 1])
        up_own = shift_z(own, 1)
        up_taken = shift_z(taken, 1)
        down_taken = shift_z(taken, -1)
        down_own = shift_z(own, -1)
        far_own = shift_z(up_own, 1)
        far_taken = shift_z(down_taken, -1)
        plus, minus, late_p, late_m, mine = product(
            info,
            (own, up_own, far_own, down_own),
            (taken, up_taken, far_taken, down_taken),
            query_grad,
            qx,
            q_other,
            qx_other,
            ahead,
        )
        from_below = shift_y(plus, 1)
        from_above = shift_y(minus, -1)
        late_p = (late_p.astype(f32) + from_below[0].astype(f32)).astype(bf16)
        late_m = (late_m.astype(f32) + from_above[1].astype(f32)).astype(bf16)
        got_p = shift_y(late_p, 1)
        got_m = shift_y(late_m, -1)
        sum_first = mine[0].astype(f32) + got_p.astype(f32) + from_above[0].astype(f32)
        sum_second = mine[1].astype(f32) + from_below[1].astype(f32) + got_m.astype(f32)
        near = jnp.stack([sum_first[:, :head_cols], sum_second[:, :head_cols]])
        other = jnp.stack([sum_first[:, head_cols:], sum_second[:, head_cols:]])
        got = swap_xl(jnp.where(same, other, near).astype(bf16))
        total = got.astype(f32) + jnp.where(same, near, other)
        done.append(total)

    grads = jnp.concatenate(done, axis=1)
    squares = sum(jnp.sum(d * d, axis=(1, 2)) for d in done)
    count = lax.axis_size("ctx") * lax.axis_size("head")
    lanes = jnp.repeat(squares, 128)[None, :]
    all_squares = lax.all_to_all(jnp.broadcast_to(lanes, (count, 256)), BOTH, 0, 0, tiled=True)

    narrow = grads.astype(bf16)
    blocks = narrow.reshape(2, NZ, NXH, owner_rows, head_cols)
    far = gather_x(jnp.where(xl == 0, blocks[:, :, 1], blocks[:, :, 0]))
    near = jnp.where(xl == 0, blocks[:, :, 0], blocks[:, :, 1])
    near = jnp.where(same, near, cross_x(near))
    flipped = cross_x(narrow)
    both = jnp.stack([near, far])
    parts = [lax.dynamic_index_in_dim(both, z, 2, False)]
    for k in range(1, NZ):
        parts.append(shift_z(lax.dynamic_index_in_dim(both, (z + k) & (NZ - 1), 2, False), k))
    facts = jnp.stack([z, xh, same.astype(z.dtype)]).astype(jnp.int32)
    return finish(facts, all_squares, parts, base, grads, flipped, ahead)


def solution(mesh):
    in_specs = (
        P("ctx", "head"),
        P("ctx", "head"),
        P("ctx"),
        P(),
        P(None, ("ctx", "head"), None),
        P(("ctx", "head"), None),
    )
    out_specs = (P(("ctx", "head"), None), P("ctx", "head"))
    return jax.shard_map(step, mesh=mesh, in_specs=in_specs, out_specs=out_specs, check_vma=False)
```

```python
import math

import jax
import jax.numpy as jnp
from jax import lax
from jax.experimental import pallas as pl
from jax.experimental.pallas import tpu as pltpu
from jax.sharding import PartitionSpec as P


clip_scale = 1.0
momentum_decay = 0.9
noise_weight = 0.8

BOTH = ("ctx", "head")
NY, NXL, NCORE, NZ, NXH = 4, 2, 2, 4, 2
CHUNKS = (144, 112)
TOKEN_BLOCK = 1024
SPLIT = 2


def lin(y, xl, core, z, xh):
    return ((y * NXL + xl) * NCORE + core) * (NZ * NXH) + z * NXH + xh


def permute(value, move):
    pairs = []
    for y in range(NY):
        for xl in range(NXL):
            for core in range(NCORE):
                for z in range(NZ):
                    for xh in range(NXH):
                        pairs.append((lin(y, xl, core, z, xh), lin(*move(y, xl, core, z, xh))))
    return lax.ppermute(value, BOTH, pairs)


def swap_core(value):
    return permute(value, lambda y, xl, core, z, xh: (y, xl, 1 - core, z, xh))


def swap_xh(value):
    return permute(value, lambda y, xl, core, z, xh: (y, xl, core, z, 1 - xh))


def swap_xl(value):
    return permute(value, lambda y, xl, core, z, xh: (y, 1 - xl, core, z, xh))


def gather_x(value):
    def move(y, xl, core, z, xh):
        to = {0: 2, 1: 0, 2: 3, 3: 1}[NXL * xh + xl]
        return y, to % NXL, core, z, to // NXL

    return permute(value, move)


def cross_x(value):
    def move(y, xl, core, z, xh):
        to = {0: 3, 1: 2, 2: 1, 3: 0}[NXL * xh + xl]
        return y, to % NXL, core, z, to // NXL

    return permute(value, move)


def shift_z(value, step):
    return permute(value, lambda y, xl, core, z, xh: (y, xl, core, (z + step) % NZ, xh))


def shift_y(value, step):
    return permute(value, lambda y, xl, core, z, xh: ((y + step) % NY, xl, core, z, xh))


def turn_kernel(core, keep, give, *outs):
    kept, given = keep[...].T, give[...].T
    start = 0
    for i, rows in enumerate(CHUNKS):
        outs[2 * i][...] = kept[start : start + rows]
        outs[2 * i + 1][...] = given[start : start + rows]
        start += rows


def turn(core, activations):
    tokens, width = activations.shape
    half = width // NCORE
    block = 1024
    shapes, specs = [], []
    for rows in CHUNKS:
        for _ in range(2):
            shapes.append(jax.ShapeDtypeStruct((rows, tokens), activations.dtype))
            specs.append(pl.BlockSpec((rows, block), lambda i, core: (0, i)))
    return pl.pallas_call(
        turn_kernel,
        grid_spec=pltpu.PrefetchScalarGridSpec(
            num_scalar_prefetch=1,
            grid=(tokens // block,),
            in_specs=[
                pl.BlockSpec((block, half), lambda i, core: (i, core[0])),
                pl.BlockSpec((block, half), lambda i, core: (i, 1 - core[0])),
            ],
            out_specs=specs,
        ),
        out_shape=shapes,
        cost_estimate=pl.CostEstimate(flops=0, bytes_accessed=4 * tokens * width, transcendentals=0),
        compiler_params=pltpu.CompilerParams(vmem_limit_bytes=60 * 1024 * 1024),
        name="turn",
    )(core, activations, activations)


def product_kernel(count_a, count_b, origin, *refs):
    sources, queries, outs = refs[0:8], refs[8:12], refs[13:20]
    left, right, total = refs[20:23]
    staged, (left_sem, right_sem, out_sem) = refs[23:30], refs[30:]
    rows = sources[0].shape[0]
    tokens, cols = queries[0].shape
    blocks = tokens // TOKEN_BLOCK

    def left_copy(half, k):
        target = left.at[half, pl.ds(k * rows, rows)]
        return pltpu.make_async_copy(sources[half * NZ + k], target, left_sem.at[half, k])

    def right_copy(half, side, j):
        at = pl.ds(j * TOKEN_BLOCK, TOKEN_BLOCK)
        source = queries[half * 2 + side].at[at]
        target = right.at[half, at, pl.ds(side * cols, cols)]
        return pltpu.make_async_copy(source, target, right_sem.at[half, side, j])

    for half in range(2):
        for k in range(NZ):
            left_copy(half, k).start()
        for j in range(blocks):
            for side in range(2):
                right_copy(half, side, j).start()

    total[...] = jnp.zeros_like(total)

    def add(half, first_count, lo, size):
        at = pl.ds(pl.multiple_of(lo, size), size)
        e = jnp.where(first_count <= lo, 1, 0)
        total[e] += jnp.dot(left[half, :, at], right[half, at, :], preferred_element_type=jnp.float32)

    def is_mixed(first_count, lo, size):
        return jnp.logical_and(first_count > lo, first_count < lo + size)

    def chunk(t, carry):
        half, j = t // blocks, t % blocks
        first_count = jnp.where(half == 0, count_a[0], count_b[0])

        @pl.when(j == 0)
        def _():
            for k in range(NZ):
                target = left.at[half, pl.ds(k * rows, rows)]
                pltpu.make_async_copy(sources[k], target, left_sem.at[half, k]).wait()

        lo = pl.multiple_of(j * TOKEN_BLOCK, TOKEN_BLOCK)
        for side in range(2):
            target = right.at[half, pl.ds(lo, TOKEN_BLOCK), pl.ds(side * cols, cols)]
            source = queries[side].at[pl.ds(lo, TOKEN_BLOCK)]
            pltpu.make_async_copy(source, target, right_sem.at[half, side, j]).wait()
        mixed = is_mixed(first_count, lo, TOKEN_BLOCK)

        @pl.when(jnp.logical_not(mixed))
        def _():
            add(half, first_count, lo, TOKEN_BLOCK)

        @pl.when(mixed)
        def _():
            size = TOKEN_BLOCK // SPLIT

            def one(i, inner_carry):
                low = lo + i * size
                at = pl.ds(pl.multiple_of(low, size), size)
                query = right[half, at, :]
                is_first = lax.broadcasted_iota(jnp.int32, query.shape, 0) < first_count - low
                nothing = jnp.zeros_like(query)
                value = left[half, :, at]

                @pl.when(first_count > low)
                def _():
                    total[0] += jnp.dot(value, jnp.where(is_first, query, nothing), preferred_element_type=jnp.float32)

                @pl.when(first_count < low + size)
                def _():
                    total[1] += jnp.dot(value, jnp.where(is_first, nothing, query), preferred_element_type=jnp.float32)

                return inner_carry

            lax.fori_loop(0, SPLIT, one, 0)

        return carry

    lax.fori_loop(0, 2 * blocks, chunk, 0)

    def block(r, e):
        k = jnp.bitwise_and(origin[0] - r, NZ - 1)
        return total[e, pl.ds(pl.multiple_of(k * rows, rows), rows), :].astype(jnp.bfloat16)

    def out_copy(i):
        return pltpu.make_async_copy(staged[i], outs[i], out_sem.at[i])

    for i, (r, e) in enumerate(((2, 0), (2, 1), (1, 1), (3, 0), (1, 0), (3, 1))):
        staged[i][...] = block(r, e)
        out_copy(i).start()
    staged[6][0] = block(0, 0)
    staged[6][1] = block(0, 1)
    out_copy(6).start()
    for i in range(7):
        out_copy(i).wait()


def product(info, left_a, left_b, q_a, qx_a, q_b, qx_b, after):
    rows, tokens = left_a[0].shape
    cols = q_a.shape[1]
    pair, single = (2, rows, 2 * cols), (rows, 2 * cols)
    shapes = [single] * 6 + [pair]
    smem = pl.BlockSpec(memory_space=pltpu.SMEM)
    anywhere = pl.BlockSpec(memory_space=pl.ANY)
    return pl.pallas_call(
        product_kernel,
        in_specs=[smem] * 3 + [anywhere] * 13,
        out_specs=[anywhere] * 7,
        out_shape=[jax.ShapeDtypeStruct(shape, jnp.bfloat16) for shape in shapes],
        scratch_shapes=[
            pltpu.VMEM((2, NZ * rows, tokens), jnp.bfloat16),
            pltpu.VMEM((2, tokens, 2 * cols), jnp.bfloat16),
            pltpu.VMEM((2, NZ * rows, 2 * cols), jnp.float32),
        ]
        + [pltpu.VMEM(shape, jnp.bfloat16) for shape in shapes]
        + [
            pltpu.SemaphoreType.DMA((2, NZ)),
            pltpu.SemaphoreType.DMA((2, 2, tokens // TOKEN_BLOCK)),
            pltpu.SemaphoreType.DMA((7,)),
        ],
        cost_estimate=pl.CostEstimate(
            flops=2 * 2 * tokens * NZ * rows * 2 * cols,
            bytes_accessed=2 * (2 * tokens * (NZ * rows + 2 * cols) + 8 * rows * 2 * cols),
            transcendentals=0,
        ),
        compiler_params=pltpu.CompilerParams(vmem_limit_bytes=28 * 1024 * 1024),
        name="product",
    )(*info, *left_a, *left_b, q_a, qx_a, q_b, qx_b, after)


def finish_kernel(
    info, squares, part_0, part_1, part_2, part_3, base, grads, flipped, ahead, momentum_new, update
):
    limit = clip_scale * math.sqrt(base.shape[1] * base.shape[1])
    sums = jnp.sum(squares[...], axis=0, keepdims=True)
    factors = limit / jnp.maximum(jnp.sqrt(sums), limit)
    cols = grads.shape[2]
    wide = [jnp.concatenate([factors[:, e * 128 : (e + 1) * 128]] * (cols // 128), axis=1) for e in range(2)]
    for k, part in enumerate((part_0, part_1, part_2, part_3)):
        origin = jnp.bitwise_and(info[0] - k, NZ - 1)
        for i, half in enumerate((info[1], 1 - info[1])):
            at = pl.ds(pl.multiple_of((origin * NXH + half) * cols, cols), cols)
            first = wide[0] * part[i, 0].astype(jnp.float32)
            second = wide[1] * part[i, 1].astype(jnp.float32)
            momentum_new[:, at] = base[:, at] + first + second

    def write(first, second):
        clipped = wide[0] * first + wide[1] * second
        total = (1.0 + momentum_decay) * clipped + ahead[...].astype(jnp.float32)
        update[...] = (-total).astype(jnp.bfloat16)

    @pl.when(info[2] == 1)
    def _():
        write(grads[0], grads[1])

    @pl.when(info[2] == 0)
    def _():
        write(flipped[0].astype(jnp.float32), flipped[1].astype(jnp.float32))


def finish(info, squares, parts, base, grads, flipped, ahead):
    return pl.pallas_call(
        finish_kernel,
        in_specs=[pl.BlockSpec(memory_space=pltpu.SMEM)] + [pl.BlockSpec(memory_space=pltpu.VMEM)] * 9,
        out_specs=[pl.BlockSpec(memory_space=pltpu.VMEM)] * 2,
        out_shape=[
            jax.ShapeDtypeStruct(base.shape, jnp.float32),
            jax.ShapeDtypeStruct(ahead.shape, jnp.bfloat16),
        ],
        compiler_params=pltpu.CompilerParams(vmem_limit_bytes=16 * 1024 * 1024),
        name="finish",
    )(info, squares, *parts, base, grads, flipped, ahead)


def step(activations, query_grad, example_ids, band_coefs, noise_history, momentum):
    f32, bf16 = jnp.float32, jnp.bfloat16
    ctx, head = lax.axis_index("ctx"), lax.axis_index("head")
    y, xl, core = ctx >> 2, (ctx >> 1) & 1, ctx & 1
    z, xh = head >> 1, head & 1
    head_cols = query_grad.shape[1]

    first_count = jnp.sum((example_ids == 0).astype(jnp.int32)).reshape(1)
    other_count = swap_core(first_count)
    info = (first_count, other_count, (z - y + NZ).reshape(1).astype(jnp.int32))

    pieces = turn(core.reshape(1).astype(jnp.int32), activations)

    qx = swap_xh(query_grad)
    q_other = swap_core(query_grad)
    qx_other = swap_core(qx)

    noise = jnp.sum(band_coefs.astype(f32)[:, None, None] * noise_history.astype(f32), axis=0)
    base = momentum_decay * momentum + noise_weight * noise
    ahead = ((1.0 + momentum_decay) * noise_weight * noise + momentum_decay**2 * momentum).astype(bf16)
    owner_rows = ahead.shape[0]
    ahead = ahead.reshape(owner_rows, NZ * NXH, head_cols).transpose(1, 0, 2)
    ahead = lax.all_to_all(ahead, "head", split_axis=0, concat_axis=0, tiled=True)
    ahead = ahead.reshape(-1, head_cols)

    same = xl == xh
    done = []
    for i in range(len(CHUNKS)):
        own = pieces[2 * i]
        taken = swap_core(pieces[2 * i + 1])
        up_own = shift_z(own, 1)
        up_taken = shift_z(taken, 1)
        down_taken = shift_z(taken, -1)
        down_own = shift_z(own, -1)
        far_own = shift_z(up_own, 1)
        far_taken = shift_z(down_taken, -1)
        far_p, far_m, near_p, near_m, late_p, late_m, mine = product(
            info,
            (own, up_own, far_own, down_own),
            (taken, up_taken, far_taken, down_taken),
            query_grad,
            qx,
            q_other,
            qx_other,
            ahead,
        )
        below_far = shift_y(far_p, 1)
        above_far = shift_y(far_m, -1)
        below_near = shift_y(near_p, 1)
        above_near = shift_y(near_m, -1)
        late_p = (late_p.astype(f32) + below_far.astype(f32)).astype(bf16)
        late_m = (late_m.astype(f32) + above_far.astype(f32)).astype(bf16)
        got_p = shift_y(late_p, 1)
        got_m = shift_y(late_m, -1)
        sum_first = mine[0].astype(f32) + got_p.astype(f32) + above_near.astype(f32)
        sum_second = mine[1].astype(f32) + below_near.astype(f32) + got_m.astype(f32)
        near = jnp.stack([sum_first[:, :head_cols], sum_second[:, :head_cols]])
        other = jnp.stack([sum_first[:, head_cols:], sum_second[:, head_cols:]])
        got = swap_xl(jnp.where(same, other, near).astype(bf16))
        total = got.astype(f32) + jnp.where(same, near, other)
        done.append(total)

    grads = jnp.concatenate(done, axis=1)
    squares = sum(jnp.sum(d * d, axis=(1, 2)) for d in done)
    count = lax.axis_size("ctx") * lax.axis_size("head")
    lanes = jnp.repeat(squares, 128)[None, :]
    all_squares = lax.all_to_all(jnp.broadcast_to(lanes, (count, 256)), BOTH, 0, 0, tiled=True)

    narrow = grads.astype(bf16)
    blocks = narrow.reshape(2, NZ, NXH, owner_rows, head_cols)
    far = gather_x(jnp.where(xl == 0, blocks[:, :, 1], blocks[:, :, 0]))
    near = jnp.where(xl == 0, blocks[:, :, 0], blocks[:, :, 1])
    near = jnp.where(same, near, cross_x(near))
    flipped = []
    for value in done:
        flipped.append(cross_x(value.astype(bf16)))
    both = jnp.stack([near, far])
    parts = [lax.dynamic_index_in_dim(both, z, 2, False)]
    for k in range(1, NZ):
        parts.append(shift_z(lax.dynamic_index_in_dim(both, (z + k) & (NZ - 1), 2, False), k))
    facts = jnp.stack([z, xh, same.astype(z.dtype)]).astype(jnp.int32)
    return finish(facts, all_squares, parts, base, grads, jnp.concatenate(flipped, axis=1), ahead)


def solution(mesh):
    in_specs = (
        P("ctx", "head"),
        P("ctx", "head"),
        P("ctx"),
        P(),
        P(None, ("ctx", "head"), None),
        P(("ctx", "head"), None),
    )
    out_specs = (P(("ctx", "head"), None), P("ctx", "head"))
    return jax.shard_map(step, mesh=mesh, in_specs=in_specs, out_specs=out_specs, check_vma=False)
```
